32 devices in a mesh: depth: 16 (over z, x, core), band: 2 (over y).
Axes of the slice: x: 2, y: 2, z: 4, core: 2. Of those that a mesh axis runs over, the one named last changes fastest.
Arguments:
- volume: int32 [64, 64, 1024], P('depth', 'band'), may hold values from 0 to 255
- tf_table: int32 [4, 256], replicated, may hold values from 0 to 255
- view_code: int32 [2, 4], replicated, may hold values from -20 to 20
Outputs:
- final_image: float32 [2, 1024, 4, 64], P(None, 'depth', None, 'band')
The draws below stay inside these ranges and needn't reach their ends.
All inputs are finite; a program needn't handle non-finite values.
Results may differ from the reference program's by a relative error of at most 0.0014.
Values may be sent and summed in bfloat16 or wider, within the bound.
A program may use at most 64 MiB of HBM per device.

```python
import jax
import jax.numpy as jnp
from jax import lax

NX = 1024
VIEWS = 2
LEVELS = 256
QMAX = 20
MARGIN = 16
NY = 64
NZ = 64


def place_ends(values, stream_key, low, high):
    index_at = [jax.random.randint(jax.random.fold_in(stream_key, axis), (), 0, length) for axis, length in enumerate(values.shape)]
    widest = values.shape.index(max(values.shape))
    next_to = index_at[:widest] + [(index_at[widest] + 1) % values.shape[widest]] + index_at[widest + 1:]
    return values.at[tuple(index_at)].set(low).at[tuple(next_to)].set(high)


def setup_inputs(seed: int = 0) -> dict:
    seeds = jax.random.split(jax.random.key(seed), 4)
    return {
        "volume": place_ends(jax.random.randint(seeds[0], (NZ, NY, NX), 0, LEVELS), jax.random.fold_in(seeds[0], 1), 0, LEVELS - 1).astype(jnp.int32),
        "tf_table": place_ends(jax.random.randint(seeds[1], (4, LEVELS), 0, 256), jax.random.fold_in(seeds[1], 1), 0, 255).astype(jnp.int32),
        "view_code": place_ends(jax.random.randint(seeds[2], (VIEWS, 4), -QMAX, QMAX + 1), jax.random.fold_in(seeds[2], 1), -QMAX, QMAX).astype(jnp.int32),
    }


tap_steps = (-2, -1, 0, 1, 2, 3)


def lanczos(offset):
    return jnp.where(jnp.abs(offset) < 3.0, jnp.sinc(offset) * jnp.sinc(offset / 3.0), 0.0)


def split_offset(coefficient, position, length, lift=0):
    numerator = coefficient * (2 * position + 1 - length) + lift * length
    integer_part = (numerator // (2 * length)).astype(jnp.int32)
    fraction = (numerator - integer_part * (2 * length)).astype(jnp.float32) / (2.0 * length)
    return integer_part, fraction


def make_palette(tf_table, depth_count):
    table_float = tf_table.astype(jnp.float32)
    opacity = table_float[3] / (64.0 * depth_count)
    premult = table_float[0:3] / 255.0 * opacity
    return jnp.concatenate([premult, opacity[None]], axis=0).astype(jnp.bfloat16)


def shear_taps(source, integer_part, fraction, along, margin):
    extent = source.shape[along]
    widths = [(0, 0)] * source.ndim
    widths[along] = (margin, margin)
    padded = jnp.pad(source.astype(jnp.float32), widths)
    accumulated = jnp.zeros(source.shape, jnp.float32)
    for step_value in tap_steps:
        tap_weight = lax.optimization_barrier(lanczos(fraction - step_value).astype(jnp.bfloat16))
        start = (margin + integer_part + step_value).astype(jnp.int32)
        shifted = lax.dynamic_slice_in_dim(padded, start, extent, along)
        accumulated = accumulated + tap_weight.astype(jnp.float32) * shifted
    return accumulated


def render(volume, palette, params):
    facing = params[3] >= 0

    def advance(picture, slice_step):
        depth_index = jnp.where(facing, slice_step, NZ - 1 - slice_step).astype(jnp.int32)
        voxels = lax.dynamic_index_in_dim(volume, depth_index, 0, keepdims=False)
        classified = jnp.take(palette, voxels, axis=1)
        whole_x, frac_x = split_offset(params[0], depth_index, NZ)
        whole_y, frac_y = split_offset(params[1], depth_index, NZ)
        row_sheared = shear_taps(classified, whole_x, frac_x, 2, MARGIN).astype(jnp.bfloat16)
        row_sheared = lax.optimization_barrier(row_sheared)
        sheared = shear_taps(row_sheared, whole_y, frac_y, 1, MARGIN)
        return picture + (1.0 - picture[3:4]) * sheared, None

    start_picture = jnp.zeros((4, NY, NX), jnp.float32)
    picture, unused = lax.scan(advance, start_picture, jnp.arange(NZ, dtype=jnp.int32))
    return picture


def warp_columns(picture, coefficient):
    columns = jnp.arange(NX, dtype=jnp.int32)
    integer_part, fraction = split_offset(coefficient, columns, NX, 1)
    accumulated = jnp.zeros(picture.shape, jnp.float32)
    for step_value in tap_steps:
        tap_weight = lanczos(fraction - step_value)
        source_index = (columns + integer_part + step_value).astype(jnp.int32)
        inside = (source_index >= 0) & (source_index < NX)
        picked = jnp.take(picture, jnp.clip(source_index, 0, NX - 1), axis=2)
        accumulated = accumulated + jnp.where(inside, tap_weight, 0.0) * picked
    return jnp.transpose(accumulated, (2, 0, 1))


def reference(volume, tf_table, view_code):
    palette = make_palette(tf_table, NZ)
    finals = []
    for view_index in range(VIEWS):
        params = view_code[view_index]
        picture = render(volume, palette, params)
        finals.append(warp_columns(picture, params[2]))
    return jnp.stack(finals)
```

```python
import functools

import jax
import jax.numpy as jnp
from jax import lax
from jax.experimental import pallas as pl
from jax.experimental.pallas import tpu as pltpu

VIEWS = 2
MARGIN = 16
PAD = 128
LANES = 128
MESH = pl.DeviceIdType.MESH


def lanczos(t):
    def sinc(u):
        x = jnp.float32(jnp.pi) * u
        safe = jnp.where(u == 0.0, 1.0, x)
        return jnp.where(u == 0.0, 1.0, jnp.sin(safe) / safe)

    return jnp.where(jnp.abs(t) < 3.0, sinc(t) * sinc(t / 3.0), 0.0)


def take(table_row, index):
    table = jnp.broadcast_to(table_row, index.shape)
    return jnp.take_along_axis(table, index, axis=1, mode="promise_in_bounds")


def replicate_alpha(part, lane):
    width = LANES // 4
    alpha = jnp.where(lane >= 3 * width, part, 0.0)
    alpha = alpha + pltpu.roll(alpha, 2 * width, 1)
    return alpha + pltpu.roll(alpha, width, 1)


def kernel(
    sizes, code_ref, volume_ref, tf_ref, out_ref,
    edge_ref, halo_ref, cls_ref, wx_ref, wy_ref, sheared_ref, picture_ref,
    s1_ref, r1_ref, s2_ref, r2_ref, k2_ref, s3_ref, r3_ref, own_ref, fin_ref,
    halo_send, halo_recv, send1, recv1, send2, recv2, send3, recv3, send4, recv4,
):
    depth_size, band_size = sizes
    slabs, rows, extent = volume_ref.shape
    wide = rows + 2 * MARGIN
    stations = depth_size // 4
    chunk = extent // stations
    strip = chunk // 4
    window = chunk + 2 * PAD
    total_depth = slabs * depth_size
    slots = 1 if band_size == 2 else 2
    d = lax.axis_index("depth")
    band = lax.axis_index("band")
    core = lax.rem(d, 2)
    col = lax.rem(lax.div(d, 2), 2)
    z = lax.div(d, 4)
    peer1 = d + 1 - 2 * core
    peer2 = d + 2 - 4 * col
    offsets = [(k + 1) // 2 if k % 2 else stations - k // 2 for k in range(1, stations)]
    offsets = sorted(offsets, key=lambda k: -min(k, stations - k)) + [0]

    def at_depth(i):
        return (i, band)

    barrier = pltpu.get_barrier_semaphore()

    def greet(device):
        pl.semaphore_signal(barrier, inc=1, device_id=device, device_id_type=MESH)

    @pl.when(band > 0)
    def _():
        greet((d, band - 1))

    @pl.when(band < band_size - 1)
    def _():
        greet((d, band + 1))

    greet(at_depth(peer1))
    greet(at_depth(peer2))
    for k in offsets[:-1]:
        greet(at_depth(lax.rem(z + k, stations) * 4 + lax.rem(d, 4)))

    @pl.when(d > 0)
    def _():
        greet(at_depth(d - 1))

    @pl.when(d < depth_size - 1)
    def _():
        greet(at_depth(d + 1))

    for s in range(slabs):
        edge_ref[0, s] = volume_ref[s, rows - MARGIN : rows, :].astype(jnp.float32).astype(jnp.bfloat16)
        edge_ref[1, s] = volume_ref[s, 0:MARGIN, :].astype(jnp.float32).astype(jnp.bfloat16)

    def neighbours(i, n):
        return lax.div(i + n - 1, n) + 1 - lax.div(i + 1, n)

    pl.semaphore_wait(
        barrier, 1 + len(offsets) + neighbours(d, depth_size) + neighbours(band, band_size))

    def to_next():
        return pltpu.make_async_remote_copy(
            edge_ref.at[0], halo_ref.at[0], halo_send.at[0], halo_recv.at[0],
            device_id=(d, lax.rem(band + 1, band_size)), device_id_type=MESH)

    def to_previous():
        last = slots - 1
        return pltpu.make_async_remote_copy(
            edge_ref.at[1], halo_ref.at[last], halo_send.at[1], halo_recv.at[last],
            device_id=(d, lax.rem(band + band_size - 1, band_size)), device_id_type=MESH)

    @pl.when(band < band_size - 1)
    def _():
        to_next().start()

    @pl.when(band > 0)
    def _():
        to_previous().start()

    table = tf_ref[...].astype(jnp.float32)
    opacity = table[3:4] / (64.0 * total_depth)
    palette = jnp.concatenate([table[0:3] / 255.0 * opacity, opacity], axis=0)
    palette = palette.astype(jnp.bfloat16).astype(jnp.float32)

    def classify(s, codes, row, lane0):
        low = codes & (LANES - 1)
        upper = codes >= LANES
        for c in range(4):
            first = take(palette[c : c + 1, 0:LANES], low)
            second = take(palette[c : c + 1, LANES : 2 * LANES], low)
            cls_ref[s, c * wide + row : c * wide + row + 16, PAD + lane0 : PAD + lane0 + LANES] = (
                jnp.where(upper, second, first).astype(jnp.bfloat16))

    def own_rows(s, carry):
        zeros = jnp.zeros((4 * wide, PAD), jnp.bfloat16)
        cls_ref[s, :, 0:PAD] = zeros
        cls_ref[s, :, PAD + extent : 2 * PAD + extent] = zeros
        for r in range(0, rows, 16):
            for x in range(0, extent, LANES):
                classify(s, volume_ref[s, r : r + 16, x : x + LANES], r, x)
        return carry

    lax.fori_loop(0, slabs, own_rows, 0)

    count = VIEWS * slabs
    row_id = lax.broadcasted_iota(jnp.int32, (2 * count, LANES), 0)
    whole = jnp.zeros((2 * count, LANES), jnp.float32)
    frac = jnp.zeros((2 * count, LANES), jnp.float32)
    period = 2 * total_depth
    for axis in range(2):
        for v in range(VIEWS):
            for s in range(slabs):
                position = d * slabs + s
                num = code_ref[v, axis] * (2 * position + 1 - total_depth)
                w = lax.div(num + 64 * period, period) - 64
                f = (num - w * period).astype(jnp.float32) / float(period)
                here = row_id == axis * count + v * slabs + s
                whole = jnp.where(here, w.astype(jnp.float32), whole)
                frac = jnp.where(here, f, frac)
    lane_f = lax.broadcasted_iota(jnp.int32, (2 * count, LANES), 1).astype(jnp.float32)
    taps = lanczos(frac - (lane_f - float(LANES // 2) - whole))

    lane16 = lax.broadcasted_iota(jnp.int32, (16, LANES), 1)
    row16 = lax.broadcasted_iota(jnp.int32, (16, LANES), 0)
    diagonal = (lane16 - row16) & (LANES - 1)
    zero_tile = jnp.zeros((16, LANES), jnp.bfloat16)
    pieces = window // LANES
    for v in range(VIEWS):
        for s in range(slabs):
            base = take(taps[v * slabs + s : v * slabs + s + 1], diagonal)
            turned = {}
            for i in range(chunk // 16):
                start = 16 * i + LANES // 2
                first, turn = start // LANES, start % LANES
                if turn not in turned:
                    moved = pltpu.roll(base, turn, 1) if turn else base
                    turned[turn] = (
                        jnp.where(lane16 >= turn, moved, 0.0).astype(jnp.bfloat16),
                        jnp.where(lane16 < turn, moved, 0.0).astype(jnp.bfloat16))
                row = v * chunk + 16 * i
                for m in range(pieces):
                    tile = turned[turn][0] if m == first else turned[turn][1] if m == first + 1 else zero_tile
                    wx_ref[s, row : row + 16, m * LANES : (m + 1) * LANES] = tile

    group = lane16 // rows
    y = lane16 - group * rows
    for v in range(VIEWS):
        for s in range(slabs):
            at = count + v * slabs + s
            for r in range(0, wide, 16):
                if r < rows:
                    position = r
                elif slots == 1 and r == rows:
                    position = jnp.where(band == 0, rows, -MARGIN)
                else:
                    position = -MARGIN if r == rows else rows
                unused = slots == 1 and r > rows
                index = row16 + position - y + LANES // 2
                tile = jnp.zeros((16, LANES), jnp.float32) if unused else take(taps[at : at + 1], index)
                for c in range(4):
                    k = c * wide + r
                    wy_ref[v * slabs + s, k : k + 16, 0:LANES] = jnp.where(group == c, tile, 0.0).astype(jnp.bfloat16)
                    wy_ref[v * slabs + s, k : k + 16, LANES : 2 * LANES] = tile.astype(jnp.bfloat16) if c == 3 else zero_tile

    @pl.when(d == 0)
    def _():
        fin_ref[:, 0:MARGIN, :] = jnp.zeros((VIEWS, MARGIN, LANES), jnp.float32)

    @pl.when(d == depth_size - 1)
    def _():
        fin_ref[:, MARGIN + strip : 2 * MARGIN + strip, :] = jnp.zeros((VIEWS, MARGIN, LANES), jnp.float32)

    has = [band > 0, band < band_size - 1] if slots == 2 else [None]
    if slots == 1:
        @pl.when(band == 0)
        def _():
            to_next().wait()

        @pl.when(band > 0)
        def _():
            to_previous().wait()
    else:
        @pl.when(band < band_size - 1)
        def _():
            to_next().wait_send()
            to_previous().wait_recv()

        @pl.when(band > 0)
        def _():
            to_previous().wait_send()
            to_next().wait_recv()

    def far_rows(s, carry):
        for slot in range(2):
            row = rows + slot * MARGIN

            def fill():
                for c in range(4):
                    cls_ref[s, c * wide + row : c * wide + row + 16, PAD : PAD + extent] = jnp.zeros((16, extent), jnp.bfloat16)

            def look():
                for x in range(0, extent, LANES):
                    codes = halo_ref[slot, s, :, x : x + LANES].astype(jnp.float32).astype(jnp.int32)
                    classify(s, codes, row, x)

            if slot >= slots:
                fill()
            elif slots == 1:
                look()
            else:
                pl.when(has[slot])(look)
                pl.when(jnp.logical_not(has[slot]))(fill)
        return carry

    lax.fori_loop(0, slabs, far_rows, 0)

    facing = [code_ref[v, 3] >= 0 for v in range(VIEWS)]
    lane_s = lax.broadcasted_iota(jnp.int32, (strip, LANES), 1)

    def over(ahead, near, far):
        front = jnp.where(ahead, near, far)
        back = jnp.where(ahead, far, near)
        return front + (1.0 - replicate_alpha(front, lane_s)) * back

    def station(step):
        return lax.rem(z + offsets[step], stations)

    def first_copy(step):
        return pltpu.make_async_remote_copy(
            s1_ref.at[step], r1_ref.at[step], send1.at[step], recv1.at[step],
            device_id=at_depth(peer1), device_id_type=MESH)

    def second_copy(step):
        return pltpu.make_async_remote_copy(
            s2_ref.at[step], r2_ref.at[step], send2.at[step], recv2.at[step],
            device_id=at_depth(peer2), device_id_type=MESH)

    def third_copy(step):
        return pltpu.make_async_remote_copy(
            s3_ref.at[step], r3_ref.at[z], send3.at[step], recv3.at[step],
            device_id=at_depth(station(step) * 4 + lax.rem(d, 4)), device_id_type=MESH)

    def render(step):
        start = pl.multiple_of(station(step) * chunk, LANES)

        def shear(s, carry):
            data = cls_ref[s, :, pl.ds(start, window)]
            moved = lax.dot_general(
                wx_ref[s], data, (((1,), (1,)), ((), ())), preferred_element_type=jnp.float32
            ).astype(jnp.bfloat16)
            for v in range(VIEWS):
                sheared_ref[v, s] = jnp.dot(
                    moved[v * chunk : (v + 1) * chunk], wy_ref[v * slabs + s],
                    preferred_element_type=jnp.float32)
            return carry

        lax.fori_loop(0, slabs, shear, 0)
        for v in range(VIEWS):
            for q in range(4):
                part = slice(q * strip, (q + 1) * strip)
                picture = None
                for k in range(slabs):
                    at = jnp.where(facing[v], slabs - 1 - k, k)
                    color = sheared_ref[v, at, part, 0:LANES]
                    if picture is None:
                        picture = color
                    else:
                        picture = color + (1.0 - sheared_ref[v, at, part, LANES : 2 * LANES]) * picture
                picture_ref[step, v, q] = picture
            for h in range(2):
                s1_ref[step, v, h] = picture_ref[step, v, 2 * h + 1 - core].astype(jnp.bfloat16)
        first_copy(step).start()

    def merge1(step):
        first_copy(step).wait()
        for v in range(VIEWS):
            ahead = (core == 0) == facing[v]
            for h, keep in ((1 - col, False), (col, True)):
                near = picture_ref[step, v, 2 * h + core]
                both = over(ahead, near, r1_ref[step, v, h].astype(jnp.float32))
                if keep:
                    k2_ref[step, v] = both
                else:
                    s2_ref[step, v] = both.astype(jnp.bfloat16)
        second_copy(step).start()

    def merge2(step):
        second_copy(step).wait()
        for v in range(VIEWS):
            ahead = (col == 0) == facing[v]
            both = over(ahead, k2_ref[step, v], r2_ref[step, v].astype(jnp.float32))
            if step == stations - 1:
                own_ref[v] = both
            else:
                s3_ref[step, v] = both.astype(jnp.bfloat16)
        if step < stations - 1:
            third_copy(step).start()

    r3_ref[z] = jnp.zeros((VIEWS, strip, LANES), jnp.bfloat16)
    for step in range(stations + 2):
        if step < stations:
            render(step)
        if 0 <= step - 1 < stations:
            merge1(step - 1)
        if 0 <= step - 2 < stations:
            merge2(step - 2)

    taps_in = strip + 2 * MARGIN
    column = lax.broadcasted_iota(jnp.int32, (strip, taps_in), 0)
    source = lax.broadcasted_iota(jnp.int32, (strip, taps_in), 1)
    double = float(2 * extent)
    weights = []
    for v in range(VIEWS):
        num = (code_ref[v, 2] * (2 * (d * strip + column) + 1 - extent) + extent).astype(jnp.float32)
        whole_w = jnp.floor(num / double)
        frac_w = (num - whole_w * double) / double
        weights.append(lanczos(frac_w - ((source - MARGIN - column).astype(jnp.float32) - whole_w)))

    for step in range(stations - 1):
        third_copy(step).wait()

    for v in range(VIEWS):
        picture = None
        for k in range(stations):
            at = jnp.where(facing[v], stations - 1 - k, k)
            part = jnp.where(at == z, own_ref[v], r3_ref[at, v].astype(jnp.float32))
            if picture is None:
                picture = part
            else:
                picture = part + (1.0 - replicate_alpha(part, lane_s)) * picture
        fin_ref[v, MARGIN : MARGIN + strip] = picture

    def to_left():
        return pltpu.make_async_remote_copy(
            fin_ref.at[:, MARGIN : 2 * MARGIN], fin_ref.at[:, MARGIN + strip : 2 * MARGIN + strip],
            send4.at[0], recv4.at[0],
            device_id=at_depth(lax.rem(d + depth_size - 1, depth_size)), device_id_type=MESH)

    def to_right():
        return pltpu.make_async_remote_copy(
            fin_ref.at[:, strip : MARGIN + strip], fin_ref.at[:, 0:MARGIN],
            send4.at[1], recv4.at[1],
            device_id=at_depth(lax.rem(d + 1, depth_size)), device_id_type=MESH)

    @pl.when(d > 0)
    def _():
        to_left().start()

    @pl.when(d < depth_size - 1)
    def _():
        to_right().start()

    @pl.when(d > 0)
    def _():
        to_left().wait_send()
        to_right().wait_recv()

    @pl.when(d < depth_size - 1)
    def _():
        to_right().wait_send()
        to_left().wait_recv()

    for v in range(VIEWS):
        out_ref[v] = jnp.dot(
            weights[v], fin_ref[v], precision=lax.Precision.HIGHEST, preferred_element_type=jnp.float32)


def body(volume, tf_table, view_code):
    depth_size, band_size = lax.axis_size("depth"), lax.axis_size("band")
    slabs, rows, extent = volume.shape
    wide = rows + 2 * MARGIN
    stations = depth_size // 4
    chunk = extent // stations
    strip = chunk // 4
    slots = 1 if band_size == 2 else 2
    bf16, f32 = jnp.bfloat16, jnp.float32
    vmem = pl.BlockSpec(memory_space=pltpu.VMEM)
    dma = pltpu.SemaphoreType.DMA
    out = pl.pallas_call(
        functools.partial(kernel, (depth_size, band_size)),
        out_shape=jax.ShapeDtypeStruct((VIEWS, strip, LANES), f32),
        in_specs=[pl.BlockSpec(memory_space=pltpu.SMEM), vmem, vmem],
        out_specs=vmem,
        scratch_shapes=[
            pltpu.VMEM((2, slabs, MARGIN, extent), bf16),
            pltpu.VMEM((slots, slabs, MARGIN, extent), bf16),
            pltpu.VMEM((slabs, 4 * wide, extent + 2 * PAD), bf16),
            pltpu.VMEM((slabs, VIEWS * chunk, chunk + 2 * PAD), bf16),
            pltpu.VMEM((VIEWS * slabs, 4 * wide, 2 * LANES), bf16),
            pltpu.VMEM((VIEWS, slabs, chunk, 2 * LANES), f32),
            pltpu.VMEM((stations, VIEWS, 4, strip, LANES), f32),
            pltpu.VMEM((stations, VIEWS, 2, strip, LANES), bf16),
            pltpu.VMEM((stations, VIEWS, 2, strip, LANES), bf16),
            pltpu.VMEM((stations, VIEWS, strip, LANES), bf16),
            pltpu.VMEM((stations, VIEWS, strip, LANES), bf16),
            pltpu.VMEM((stations, VIEWS, strip, LANES), f32),
            pltpu.VMEM((stations, VIEWS, strip, LANES), bf16),
            pltpu.VMEM((stations, VIEWS, strip, LANES), bf16),
            pltpu.VMEM((VIEWS, strip, LANES), f32),
            pltpu.VMEM((VIEWS, strip + 2 * MARGIN, LANES), f32),
            dma((2,)), dma((slots,)),
            dma((stations,)), dma((stations,)),
            dma((stations,)), dma((stations,)),
            dma((stations,)), dma((stations,)),
            dma((2,)), dma((2,)),
        ],
        compiler_params=pltpu.CompilerParams(collective_id=0, has_side_effects=True),
    )(view_code, volume, tf_table)
    return out.reshape(VIEWS, strip, 4, rows)


def solution(mesh):
    P = jax.sharding.PartitionSpec
    placed = (P("depth", "band", None), P(), P())
    return jax.shard_map(
        body, mesh=mesh, in_specs=placed, out_specs=P(None, "depth", None, "band"), check_vma=False
    )
```

```python
import functools

import jax
import jax.numpy as jnp
from jax import lax
from jax.experimental import pallas as pl
from jax.experimental.pallas import tpu as pltpu

VIEWS = 2
MARGIN = 16
PAD = 128
LANES = 128
MESH = pl.DeviceIdType.MESH


def lanczos(t):
    def sinc(u):
        x = jnp.float32(jnp.pi) * u
        safe = jnp.where(u == 0.0, 1.0, x)
        return jnp.where(u == 0.0, 1.0, jnp.sin(safe) / safe)

    return jnp.where(jnp.abs(t) < 3.0, sinc(t) * sinc(t / 3.0), 0.0)


def take(table_row, index):
    table = jnp.broadcast_to(table_row, index.shape)
    return jnp.take_along_axis(table, index, axis=1, mode="promise_in_bounds")


def replicate_alpha(part, lane):
    width = LANES // 4
    alpha = jnp.where(lane >= 3 * width, part, 0.0)
    alpha = alpha + pltpu.roll(alpha, 2 * width, 1)
    return alpha + pltpu.roll(alpha, width, 1)


def kernel(
    sizes, code_ref, volume_ref, tf_ref, out_ref,
    edge_ref, halo_ref, cls_ref, wx_ref, wy_ref, sheared_ref, picture_ref,
    s1_ref, r1_ref, s2_ref, r2_ref, k2_ref, s3_ref, r3_ref, own_ref,
    halo_send, halo_recv, send1, recv1, send2, recv2, send3, recv3,
):
    depth_size, band_size = sizes
    slabs, rows, extent = volume_ref.shape
    wide = rows + 2 * MARGIN
    stations = depth_size // 4
    chunk = extent // stations
    strip = chunk // 4
    window = chunk + 2 * PAD
    reach = chunk + 2 * MARGIN
    piece = strip + 2 * MARGIN
    total_depth = slabs * depth_size
    slots = 1 if band_size == 2 else 2
    d = lax.axis_index("depth")
    band = lax.axis_index("band")
    core = lax.rem(d, 2)
    col = lax.rem(lax.div(d, 2), 2)
    z = lax.div(d, 4)
    peer1 = d + 1 - 2 * core
    peer2 = d + 2 - 4 * col
    offsets = [(k + 1) // 2 if k % 2 else stations - k // 2 for k in range(1, stations)]
    offsets = sorted(offsets, key=lambda k: -min(k, stations - k)) + [0]

    def at_depth(i):
        return (i, band)

    barrier = pltpu.get_barrier_semaphore()

    def greet(device):
        pl.semaphore_signal(barrier, inc=1, device_id=device, device_id_type=MESH)

    @pl.when(band > 0)
    def _():
        greet((d, band - 1))

    @pl.when(band < band_size - 1)
    def _():
        greet((d, band + 1))

    greet(at_depth(peer1))
    greet(at_depth(peer2))
    for k in offsets[:-1]:
        greet(at_depth(lax.rem(z + k, stations) * 4 + lax.rem(d, 4)))

    for s in range(slabs):
        edge_ref[0, s] = volume_ref[s, rows - MARGIN : rows, :].astype(jnp.float32).astype(jnp.bfloat16)
        edge_ref[1, s] = volume_ref[s, 0:MARGIN, :].astype(jnp.float32).astype(jnp.bfloat16)

    def neighbours(i, n):
        return lax.div(i + n - 1, n) + 1 - lax.div(i + 1, n)

    pl.semaphore_wait(
        barrier, 1 + len(offsets) + neighbours(band, band_size))

    def to_next():
        return pltpu.make_async_remote_copy(
            edge_ref.at[0], halo_ref.at[0], halo_send.at[0], halo_recv.at[0],
            device_id=(d, lax.rem(band + 1, band_size)), device_id_type=MESH)

    def to_previous():
        last = slots - 1
        return pltpu.make_async_remote_copy(
            edge_ref.at[1], halo_ref.at[last], halo_send.at[1], halo_recv.at[last],
            device_id=(d, lax.rem(band + band_size - 1, band_size)), device_id_type=MESH)

    @pl.when(band < band_size - 1)
    def _():
        to_next().start()

    @pl.when(band > 0)
    def _():
        to_previous().start()

    table = tf_ref[...].astype(jnp.float32)
    opacity = table[3:4] / (64.0 * total_depth)
    palette = jnp.concatenate([table[0:3] / 255.0 * opacity, opacity], axis=0)
    palette = palette.astype(jnp.bfloat16).astype(jnp.float32)

    def classify(s, codes, row, lane0):
        low = codes & (LANES - 1)
        upper = codes >= LANES
        for c in range(4):
            first = take(palette[c : c + 1, 0:LANES], low)
            second = take(palette[c : c + 1, LANES : 2 * LANES], low)
            cls_ref[s, c * wide + row : c * wide + row + 16, PAD + lane0 : PAD + lane0 + LANES] = (
                jnp.where(upper, second, first).astype(jnp.bfloat16))

    def own_rows(s, carry):
        zeros = jnp.zeros((4 * wide, PAD), jnp.bfloat16)
        cls_ref[s, :, 0:PAD] = zeros
        cls_ref[s, :, PAD + extent : 2 * PAD + extent] = zeros
        for r in range(0, rows, 16):
            for x in range(0, extent, LANES):
                classify(s, volume_ref[s, r : r + 16, x : x + LANES], r, x)
        return carry

    lax.fori_loop(0, slabs, own_rows, 0)

    count = VIEWS * slabs
    row_id = lax.broadcasted_iota(jnp.int32, (2 * count, LANES), 0)
    whole = jnp.zeros((2 * count, LANES), jnp.float32)
    frac = jnp.zeros((2 * count, LANES), jnp.float32)
    period = 2 * total_depth
    for axis in range(2):
        for v in range(VIEWS):
            for s in range(slabs):
                position = d * slabs + s
                num = code_ref[v, axis] * (2 * position + 1 - total_depth)
                w = lax.div(num + 64 * period, period) - 64
                f = (num - w * period).astype(jnp.float32) / float(period)
                here = row_id == axis * count + v * slabs + s
                whole = jnp.where(here, w.astype(jnp.float32), whole)
                frac = jnp.where(here, f, frac)
    lane_f = lax.broadcasted_iota(jnp.int32, (2 * count, LANES), 1).astype(jnp.float32)
    taps = lanczos(frac - (lane_f - float(LANES // 2) - whole))

    lane16 = lax.broadcasted_iota(jnp.int32, (16, LANES), 1)
    row16 = lax.broadcasted_iota(jnp.int32, (16, LANES), 0)
    diagonal = (lane16 - row16) & (LANES - 1)
    zero_tile = jnp.zeros((16, LANES), jnp.bfloat16)
    pieces = window // LANES
    for v in range(VIEWS):
        for s in range(slabs):
            base = take(taps[v * slabs + s : v * slabs + s + 1], diagonal)
            turned = {}
            for i in range(reach // 16):
                start = 16 * i - MARGIN + LANES // 2
                first, turn = start // LANES, start % LANES
                if turn not in turned:
                    moved = pltpu.roll(base, turn, 1) if turn else base
                    turned[turn] = (
                        jnp.where(lane16 >= turn, moved, 0.0).astype(jnp.bfloat16),
                        jnp.where(lane16 < turn, moved, 0.0).astype(jnp.bfloat16))
                row = v * reach + 16 * i
                for m in range(pieces):
                    tile = turned[turn][0] if m == first else turned[turn][1] if m == first + 1 else zero_tile
                    wx_ref[s, row : row + 16, m * LANES : (m + 1) * LANES] = tile

    group = lane16 // rows
    y = lane16 - group * rows
    for v in range(VIEWS):
        for s in range(slabs):
            at = count + v * slabs + s
            for r in range(0, wide, 16):
                if r < rows:
                    position = r
                elif slots == 1 and r == rows:
                    position = jnp.where(band == 0, rows, -MARGIN)
                else:
                    position = -MARGIN if r == rows else rows
                unused = slots == 1 and r > rows
                index = row16 + position - y + LANES // 2
                tile = jnp.zeros((16, LANES), jnp.float32) if unused else take(taps[at : at + 1], index)
                for c in range(4):
                    k = c * wide + r
                    wy_ref[v * slabs + s, k : k + 16, 0:LANES] = jnp.where(group == c, tile, 0.0).astype(jnp.bfloat16)
                    wy_ref[v * slabs + s, k : k + 16, LANES : 2 * LANES] = tile.astype(jnp.bfloat16) if c == 3 else zero_tile

    has = [band > 0, band < band_size - 1] if slots == 2 else [None]
    if slots == 1:
        @pl.when(band == 0)
        def _():
            to_next().wait()

        @pl.when(band > 0)
        def _():
            to_previous().wait()
    else:
        @pl.when(band < band_size - 1)
        def _():
            to_next().wait_send()
            to_previous().wait_recv()

        @pl.when(band > 0)
        def _():
            to_previous().wait_send()
            to_next().wait_recv()

    def far_rows(s, carry):
        for slot in range(2):
            row = rows + slot * MARGIN

            def fill():
                for c in range(4):
                    cls_ref[s, c * wide + row : c * wide + row + 16, PAD : PAD + extent] = jnp.zeros((16, extent), jnp.bfloat16)

            def look():
                for x in range(0, extent, LANES):
                    codes = halo_ref[slot, s, :, x : x + LANES].astype(jnp.float32).astype(jnp.int32)
                    classify(s, codes, row, x)

            if slot >= slots:
                fill()
            elif slots == 1:
                look()
            else:
                pl.when(has[slot])(look)
                pl.when(jnp.logical_not(has[slot]))(fill)
        return carry

    lax.fori_loop(0, slabs, far_rows, 0)

    facing = [code_ref[v, 3] >= 0 for v in range(VIEWS)]
    lane_s = lax.broadcasted_iota(jnp.int32, (piece, LANES), 1)

    def over(ahead, near, far):
        front = jnp.where(ahead, near, far)
        back = jnp.where(ahead, far, near)
        return front + (1.0 - replicate_alpha(front, lane_s)) * back

    def station(step):
        return lax.rem(z + offsets[step], stations)

    def first_copy(step):
        return pltpu.make_async_remote_copy(
            s1_ref.at[step], r1_ref.at[step], send1.at[step], recv1.at[step],
            device_id=at_depth(peer1), device_id_type=MESH)

    def second_copy(step):
        return pltpu.make_async_remote_copy(
            s2_ref.at[step], r2_ref.at[step], send2.at[step], recv2.at[step],
            device_id=at_depth(peer2), device_id_type=MESH)

    def third_copy(step):
        return pltpu.make_async_remote_copy(
            s3_ref.at[step], r3_ref.at[z], send3.at[step], recv3.at[step],
            device_id=at_depth(station(step) * 4 + lax.rem(d, 4)), device_id_type=MESH)

    def strip_of(step, v, q):
        return picture_ref[step, v, pl.ds(pl.multiple_of(q * strip, 16), piece), :]

    def render(step):
        start = pl.multiple_of(station(step) * chunk, LANES)

        def shear(s, carry):
            data = cls_ref[s, :, pl.ds(start, window)]
            moved = lax.dot_general(
                wx_ref[s], data, (((1,), (1,)), ((), ())), preferred_element_type=jnp.float32
            ).astype(jnp.bfloat16)
            for v in range(VIEWS):
                sheared_ref[v, s] = jnp.dot(
                    moved[v * reach : (v + 1) * reach], wy_ref[v * slabs + s],
                    preferred_element_type=jnp.float32)
            return carry

        lax.fori_loop(0, slabs, shear, 0, unroll=True)
        for v in range(VIEWS):
            for q in range(0, reach, 32):
                part = slice(q, q + 32)
                picture = None
                for k in range(slabs):
                    at = jnp.where(facing[v], slabs - 1 - k, k)
                    color = sheared_ref[v, at, part, 0:LANES]
                    if picture is None:
                        picture = color
                    else:
                        picture = color + (1.0 - sheared_ref[v, at, part, LANES : 2 * LANES]) * picture
                picture_ref[step, v, part] = picture
            for h in range(2):
                s1_ref[step, v, h] = strip_of(step, v, 2 * h + 1 - core).astype(jnp.bfloat16)
        first_copy(step).start()

    def merge1(step):
        first_copy(step).wait()
        for v in range(VIEWS):
            ahead = (core == 0) == facing[v]
            for h, keep in ((1 - col, False), (col, True)):
                near = strip_of(step, v, 2 * h + core)
                both = over(ahead, near, r1_ref[step, v, h].astype(jnp.float32))
                if keep:
                    k2_ref[step, v] = both
                else:
                    s2_ref[step, v] = both.astype(jnp.bfloat16)
        second_copy(step).start()

    def merge2(step):
        second_copy(step).wait()
        for v in range(VIEWS):
            ahead = (col == 0) == facing[v]
            both = over(ahead, k2_ref[step, v], r2_ref[step, v].astype(jnp.float32))
            if step == stations - 1:
                own_ref[v] = both
            else:
                s3_ref[step, v] = both.astype(jnp.bfloat16)
        if step < stations - 1:
            third_copy(step).start()

    r3_ref[z] = jnp.zeros((VIEWS, piece, LANES), jnp.bfloat16)
    for step in range(stations + 2):
        if step < stations:
            render(step)
        if 0 <= step - 1 < stations:
            merge1(step - 1)
        if 0 <= step - 2 < stations:
            merge2(step - 2)

    taps_in = piece
    column = lax.broadcasted_iota(jnp.int32, (strip, taps_in), 0)
    source = lax.broadcasted_iota(jnp.int32, (strip, taps_in), 1)
    double = float(2 * extent)
    column_in = d * strip + source - MARGIN
    inside = jnp.logical_and(column_in >= 0, column_in < extent)
    weights = []
    for v in range(VIEWS):
        num = (code_ref[v, 2] * (2 * (d * strip + column) + 1 - extent) + extent).astype(jnp.float32)
        whole_w = jnp.floor(num / double)
        frac_w = (num - whole_w * double) / double
        tap = lanczos(frac_w - ((source - MARGIN - column).astype(jnp.float32) - whole_w))
        weights.append(jnp.where(inside, tap, 0.0))

    for step in range(stations - 1):
        third_copy(step).wait()

    for v in range(VIEWS):
        picture = None
        for k in range(stations):
            at = jnp.where(facing[v], stations - 1 - k, k)
            part = jnp.where(at == z, own_ref[v], r3_ref[at, v].astype(jnp.float32))
            if picture is None:
                picture = part
            else:
                picture = part + (1.0 - replicate_alpha(part, lane_s)) * picture
        final = jnp.dot(
            weights[v], picture, precision=lax.Precision.HIGHEST, preferred_element_type=jnp.float32)
        out_ref[v] = final.T


def body(volume, tf_table, view_code):
    depth_size, band_size = lax.axis_size("depth"), lax.axis_size("band")
    slabs, rows, extent = volume.shape
    wide = rows + 2 * MARGIN
    stations = depth_size // 4
    chunk = extent // stations
    strip = chunk // 4
    reach = chunk + 2 * MARGIN
    piece = strip + 2 * MARGIN
    slots = 1 if band_size == 2 else 2
    bf16, f32 = jnp.bfloat16, jnp.float32
    vmem = pl.BlockSpec(memory_space=pltpu.VMEM)
    dma = pltpu.SemaphoreType.DMA
    out = pl.pallas_call(
        functools.partial(kernel, (depth_size, band_size)),
        out_shape=jax.ShapeDtypeStruct((VIEWS, LANES, strip), f32),
        in_specs=[pl.BlockSpec(memory_space=pltpu.SMEM), vmem, vmem],
        out_specs=vmem,
        scratch_shapes=[
            pltpu.VMEM((2, slabs, MARGIN, extent), bf16),
            pltpu.VMEM((slots, slabs, MARGIN, extent), bf16),
            pltpu.VMEM((slabs, 4 * wide, extent + 2 * PAD), bf16),
            pltpu.VMEM((slabs, VIEWS * reach, chunk + 2 * PAD), bf16),
            pltpu.VMEM((VIEWS * slabs, 4 * wide, 2 * LANES), bf16),
            pltpu.VMEM((VIEWS, slabs, reach, 2 * LANES), f32),
            pltpu.VMEM((stations, VIEWS, reach, LANES), f32),
            pltpu.VMEM((stations, VIEWS, 2, piece, LANES), bf16),
            pltpu.VMEM((stations, VIEWS, 2, piece, LANES), bf16),
            pltpu.VMEM((stations, VIEWS, piece, LANES), bf16),
            pltpu.VMEM((stations, VIEWS, piece, LANES), bf16),
            pltpu.VMEM((stations, VIEWS, piece, LANES), f32),
            pltpu.VMEM((stations, VIEWS, piece, LANES), bf16),
            pltpu.VMEM((stations, VIEWS, piece, LANES), bf16),
            pltpu.VMEM((VIEWS, piece, LANES), f32),
            dma((2,)), dma((slots,)),
            dma((stations,)), dma((stations,)),
            dma((stations,)), dma((stations,)),
            dma((stations,)), dma((stations,)),
        ],
        compiler_params=pltpu.CompilerParams(collective_id=0, has_side_effects=True),
    )(view_code, volume, tf_table)
    return out.reshape(VIEWS, 4, rows, strip).transpose(0, 3, 1, 2)


def solution(mesh):
    P = jax.sharding.PartitionSpec
    placed = (P("depth", "band", None), P(), P())
    return jax.shard_map(
        body, mesh=mesh, in_specs=placed, out_specs=P(None, "depth", None, "band"), check_vma=False
    )
```

```python
import functools

import jax
import jax.numpy as jnp
from jax import lax
from jax.experimental import pallas as pl
from jax.experimental.pallas import tpu as pltpu

VIEWS = 2
MARGIN = 16
PAD = 128
LANES = 128
MESH = pl.DeviceIdType.MESH


def lanczos(t):
    def sinc(u):
        x = jnp.float32(jnp.pi) * u
        safe = jnp.where(u == 0.0, 1.0, x)
        return jnp.where(u == 0.0, 1.0, jnp.sin(safe) / safe)

    return jnp.where(jnp.abs(t) < 3.0, sinc(t) * sinc(t / 3.0), 0.0)


def take(table_row, index):
    table = jnp.broadcast_to(table_row, index.shape)
    return jnp.take_along_axis(table, index, axis=1, mode="promise_in_bounds")


def replicate_alpha(part, lane):
    width = LANES // 4
    alpha = jnp.where(lane >= 3 * width, part, 0.0)
    alpha = alpha + pltpu.roll(alpha, 2 * width, 1)
    return alpha + pltpu.roll(alpha, width, 1)


def kernel(
    sizes, code_ref, volume_ref, tf_ref, out_ref,
    edge_ref, halo_ref, cls_ref, wx_ref, wy_ref, sheared_ref, picture_ref,
    s1_ref, r1_ref, s2_ref, r2_ref, k2_ref, s3_ref, r3_ref, own_ref,
    halo_send, halo_recv, send1, recv1, send2, recv2, send3, recv3,
):
    depth_size, band_size = sizes
    slabs, rows, extent = volume_ref.shape
    wide = rows + 2 * MARGIN
    stations = depth_size // 4
    chunk = extent // stations
    strip = chunk // 4
    window = chunk + 2 * PAD
    reach = chunk + 2 * MARGIN
    piece = strip + 2 * MARGIN
    total_depth = slabs * depth_size
    slots = 1 if band_size == 2 else 2
    d = lax.axis_index("depth")
    band = lax.axis_index("band")
    core = lax.rem(d, 2)
    col = lax.rem(lax.div(d, 2), 2)
    z = lax.div(d, 4)
    peer1 = d + 1 - 2 * core
    peer2 = d + 2 - 4 * col
    half = stations // 2
    low = 1 - lax.div(z, half)

    def mirrored(i):
        return i * low + (stations - 1 - i) * (1 - low)

    def station(step):
        if step < half:
            return mirrored(stations - 1 - step)
        if step == stations - 1:
            return z
        u, inner = step - half, half - 1 - mirrored(z)
        return mirrored(jnp.where(u < inner, half - 1 - u, u - inner))

    def at_depth(i):
        return (i, band)

    barrier = pltpu.get_barrier_semaphore()

    def greet(device):
        pl.semaphore_signal(barrier, inc=1, device_id=device, device_id_type=MESH)

    @pl.when(band > 0)
    def _():
        greet((d, band - 1))

    @pl.when(band < band_size - 1)
    def _():
        greet((d, band + 1))

    greet(at_depth(peer1))
    greet(at_depth(peer2))
    for k in range(1, stations):
        greet(at_depth(lax.rem(z + k, stations) * 4 + lax.rem(d, 4)))

    for s in range(slabs):
        edge_ref[0, s] = volume_ref[s, rows - MARGIN : rows, :].astype(jnp.float32).astype(jnp.bfloat16)
        edge_ref[1, s] = volume_ref[s, 0:MARGIN, :].astype(jnp.float32).astype(jnp.bfloat16)

    def neighbours(i, n):
        return lax.div(i + n - 1, n) + 1 - lax.div(i + 1, n)

    pl.semaphore_wait(
        barrier, 1 + stations + neighbours(band, band_size))

    units, near_units = extent // LANES, chunk // LANES + 1
    cuts = ((units - near_units, units), (units // 2 - 1, units - near_units), (0, units // 2 - 1))

    def lanes_of(g):
        first, last = cuts[g]
        start = first * low + (units - last) * (1 - low)
        return pl.multiple_of(start * LANES, LANES), last - first

    def group_of(ref, slot, g):
        start, width = lanes_of(g)
        return ref.at[slot, :, :, pl.ds(start, width * LANES)]

    def to_next(g):
        return pltpu.make_async_remote_copy(
            group_of(edge_ref, 0, g), group_of(halo_ref, 0, g), halo_send.at[0, g], halo_recv.at[0, g],
            device_id=(d, lax.rem(band + 1, band_size)), device_id_type=MESH)

    def to_previous(g):
        last = slots - 1
        return pltpu.make_async_remote_copy(
            group_of(edge_ref, 1, g), group_of(halo_ref, last, g), halo_send.at[1, g], halo_recv.at[last, g],
            device_id=(d, lax.rem(band + band_size - 1, band_size)), device_id_type=MESH)

    @pl.when(band < band_size - 1)
    def _():
        for g in range(3):
            to_next(g).start()

    @pl.when(band > 0)
    def _():
        for g in range(3):
            to_previous(g).start()

    table = tf_ref[...].astype(jnp.float32)
    opacity = table[3:4] / (64.0 * total_depth)
    palette = jnp.concatenate([table[0:3] / 255.0 * opacity, opacity], axis=0)
    palette = palette.astype(jnp.bfloat16).astype(jnp.float32)

    def classify(s, codes, row, lane0):
        low = codes & (LANES - 1)
        upper = codes >= LANES
        for c in range(4):
            first = take(palette[c : c + 1, 0:LANES], low)
            second = take(palette[c : c + 1, LANES : 2 * LANES], low)
            cls_ref[s, c * wide + row : c * wide + row + 16, pl.ds(PAD + lane0, LANES)] = (
                jnp.where(upper, second, first).astype(jnp.bfloat16))

    def own_rows(s, carry):
        zeros = jnp.zeros((4 * wide, PAD), jnp.bfloat16)
        cls_ref[s, :, 0:PAD] = zeros
        cls_ref[s, :, PAD + extent : 2 * PAD + extent] = zeros
        for r in range(0, rows, 16):
            for x in range(0, extent, LANES):
                classify(s, volume_ref[s, r : r + 16, x : x + LANES], r, x)
        return carry

    lax.fori_loop(0, slabs, own_rows, 0)

    count = VIEWS * slabs
    row_id = lax.broadcasted_iota(jnp.int32, (2 * count, LANES), 0)
    whole = jnp.zeros((2 * count, LANES), jnp.float32)
    frac = jnp.zeros((2 * count, LANES), jnp.float32)
    period = 2 * total_depth
    for axis in range(2):
        for v in range(VIEWS):
            for s in range(slabs):
                position = d * slabs + s
                num = code_ref[v, axis] * (2 * position + 1 - total_depth)
                w = lax.div(num + 64 * period, period) - 64
                f = (num - w * period).astype(jnp.float32) / float(period)
                here = row_id == axis * count + v * slabs + s
                whole = jnp.where(here, w.astype(jnp.float32), whole)
                frac = jnp.where(here, f, frac)
    lane_f = lax.broadcasted_iota(jnp.int32, (2 * count, LANES), 1).astype(jnp.float32)
    taps = lanczos(frac - (lane_f - float(LANES // 2) - whole))

    lane16 = lax.broadcasted_iota(jnp.int32, (16, LANES), 1)
    row16 = lax.broadcasted_iota(jnp.int32, (16, LANES), 0)
    diagonal = (lane16 - row16) & (LANES - 1)
    zero_tile = jnp.zeros((16, LANES), jnp.bfloat16)
    pieces = window // LANES
    for v in range(VIEWS):
        for s in range(slabs):
            base = take(taps[v * slabs + s : v * slabs + s + 1], diagonal)
            turned = {}
            for i in range(reach // 16):
                start = 16 * i - MARGIN + LANES // 2
                first, turn = start // LANES, start % LANES
                if turn not in turned:
                    moved = pltpu.roll(base, turn, 1) if turn else base
                    turned[turn] = (
                        jnp.where(lane16 >= turn, moved, 0.0).astype(jnp.bfloat16),
                        jnp.where(lane16 < turn, moved, 0.0).astype(jnp.bfloat16))
                row = v * reach + 16 * i
                for m in range(pieces):
                    tile = turned[turn][0] if m == first else turned[turn][1] if m == first + 1 else zero_tile
                    wx_ref[s, row : row + 16, m * LANES : (m + 1) * LANES] = tile

    group = lane16 // rows
    y = lane16 - group * rows
    for v in range(VIEWS):
        for s in range(slabs):
            at = count + v * slabs + s
            for r in range(0, wide, 16):
                if r < rows:
                    position = r
                elif slots == 1 and r == rows:
                    position = jnp.where(band == 0, rows, -MARGIN)
                else:
                    position = -MARGIN if r == rows else rows
                unused = slots == 1 and r > rows
                index = row16 + position - y + LANES // 2
                tile = jnp.zeros((16, LANES), jnp.float32) if unused else take(taps[at : at + 1], index)
                for c in range(4):
                    k = c * wide + r
                    wy_ref[v * slabs + s, k : k + 16, 0:LANES] = jnp.where(group == c, tile, 0.0).astype(jnp.bfloat16)
                    wy_ref[v * slabs + s, k : k + 16, LANES : 2 * LANES] = tile.astype(jnp.bfloat16) if c == 3 else zero_tile

    has = [band > 0, band < band_size - 1] if slots == 2 else [None]
    def clear(slot):
        row = rows + slot * MARGIN
        for s in range(slabs):
            for c in range(4):
                cls_ref[s, c * wide + row : c * wide + row + 16, PAD : PAD + extent] = jnp.zeros((16, extent), jnp.bfloat16)

    for slot in range(2):
        if slot >= slots:
            clear(slot)
        elif slots == 2:
            pl.when(jnp.logical_not(has[slot]))(functools.partial(clear, slot))

    def far_rows(g):
        if slots == 1:
            @pl.when(band == 0)
            def _():
                to_next(g).wait()

            @pl.when(band > 0)
            def _():
                to_previous(g).wait()
        else:
            @pl.when(band < band_size - 1)
            def _():
                to_next(g).wait_send()
                to_previous(g).wait_recv()

            @pl.when(band > 0)
            def _():
                to_previous(g).wait_send()
                to_next(g).wait_recv()

        start, width = lanes_of(g)

        def look(slot):
            for s in range(slabs):
                for i in range(width):
                    x = pl.multiple_of(start + i * LANES, LANES)
                    codes = halo_ref[slot, s, :, pl.ds(x, LANES)].astype(jnp.float32).astype(jnp.int32)
                    classify(s, codes, rows + slot * MARGIN, x)

        for slot in range(slots):
            if slots == 1:
                look(slot)
            else:
                pl.when(has[slot])(functools.partial(look, slot))

    facing = [code_ref[v, 3] >= 0 for v in range(VIEWS)]
    lane_s = lax.broadcasted_iota(jnp.int32, (piece, LANES), 1)

    def over(ahead, near, far):
        front = jnp.where(ahead, near, far)
        back = jnp.where(ahead, far, near)
        return front + (1.0 - replicate_alpha(front, lane_s)) * back

    def first_copy(step):
        return pltpu.make_async_remote_copy(
            s1_ref.at[step], r1_ref.at[step], send1.at[step], recv1.at[step],
            device_id=at_depth(peer1), device_id_type=MESH)

    def second_copy(step):
        return pltpu.make_async_remote_copy(
            s2_ref.at[step], r2_ref.at[step], send2.at[step], recv2.at[step],
            device_id=at_depth(peer2), device_id_type=MESH)

    def third_copy(step):
        return pltpu.make_async_remote_copy(
            s3_ref.at[step], r3_ref.at[z], send3.at[step], recv3.at[z],
            device_id=at_depth(station(step) * 4 + lax.rem(d, 4)), device_id_type=MESH)

    def strip_of(step, v, q):
        return picture_ref[step, v, pl.ds(pl.multiple_of(q * strip, 16), piece), :]

    def render(step):
        start = pl.multiple_of(station(step) * chunk, LANES)

        def shear(s, carry):
            data = cls_ref[s, :, pl.ds(start, window)]
            moved = lax.dot_general(
                wx_ref[s], data, (((1,), (1,)), ((), ())), preferred_element_type=jnp.float32
            ).astype(jnp.bfloat16)
            for v in range(VIEWS):
                sheared_ref[v, s] = jnp.dot(
                    moved[v * reach : (v + 1) * reach], wy_ref[v * slabs + s],
                    preferred_element_type=jnp.float32)
            return carry

        for s in range(slabs):
            shear(s, 0)
            if s == slabs // 2 - 1 and step > 0:
                merge1(step - 1)
        for v in range(VIEWS):
            for q in range(0, reach, 32):
                part = slice(q, q + 32)
                picture = None
                for k in range(slabs):
                    at = jnp.where(facing[v], slabs - 1 - k, k)
                    color = sheared_ref[v, at, part, 0:LANES]
                    if picture is None:
                        picture = color
                    else:
                        picture = color + (1.0 - sheared_ref[v, at, part, LANES : 2 * LANES]) * picture
                picture_ref[step, v, part] = picture
            for h in range(2):
                s1_ref[step, v, h] = strip_of(step, v, 2 * h + 1 - core).astype(jnp.bfloat16)
        first_copy(step).start()

    def merge1(step):
        first_copy(step).wait()
        for v in range(VIEWS):
            ahead = (core == 0) == facing[v]
            for h, keep in ((1 - col, False), (col, True)):
                near = strip_of(step, v, 2 * h + core)
                both = over(ahead, near, r1_ref[step, v, h].astype(jnp.float32))
                if keep:
                    k2_ref[step, v] = both
                else:
                    s2_ref[step, v] = both.astype(jnp.bfloat16)
        second_copy(step).start()

    def merge2(step):
        second_copy(step).wait()
        for v in range(VIEWS):
            ahead = (col == 0) == facing[v]
            both = over(ahead, k2_ref[step, v], r2_ref[step, v].astype(jnp.float32))
            if step == stations - 1:
                own_ref[v] = both
            else:
                s3_ref[step, v] = both.astype(jnp.bfloat16)
        if step < stations - 1:
            third_copy(step).start()

    r3_ref[z] = jnp.zeros((VIEWS, piece, LANES), jnp.bfloat16)
    for step in range(stations + 2):
        if step < stations:
            if step in (0, 1, half):
                far_rows((0, 1, half).index(step))
            render(step)
        if step == stations:
            merge1(step - 1)
        if 0 <= step - 2 < stations:
            merge2(step - 2)

    taps_in = piece
    column = lax.broadcasted_iota(jnp.int32, (strip, taps_in), 0)
    source = lax.broadcasted_iota(jnp.int32, (strip, taps_in), 1)
    double = float(2 * extent)
    column_in = d * strip + source - MARGIN
    inside = jnp.logical_and(column_in >= 0, column_in < extent)
    weights = []
    for v in range(VIEWS):
        num = (code_ref[v, 2] * (2 * (d * strip + column) + 1 - extent) + extent).astype(jnp.float32)
        whole_w = jnp.floor(num / double)
        frac_w = (num - whole_w * double) / double
        tap = lanczos(frac_w - ((source - MARGIN - column).astype(jnp.float32) - whole_w))
        weights.append(jnp.where(inside, tap, 0.0))

    for step in range(stations - 1):
        third_copy(step).wait_send()
    for k in range(1, stations):
        other = lax.rem(z + k, stations)
        pltpu.make_async_remote_copy(
            s3_ref.at[0], r3_ref.at[other], send3.at[0], recv3.at[other],
            device_id=at_depth(other * 4 + lax.rem(d, 4)), device_id_type=MESH).wait_recv()

    for v in range(VIEWS):
        picture = None
        for k in range(stations):
            at = jnp.where(facing[v], stations - 1 - k, k)
            part = jnp.where(at == z, own_ref[v], r3_ref[at, v].astype(jnp.float32))
            if picture is None:
                picture = part
            else:
                picture = part + (1.0 - replicate_alpha(part, lane_s)) * picture
        final = jnp.dot(
            weights[v], picture, precision=lax.Precision.HIGHEST, preferred_element_type=jnp.float32)
        out_ref[v] = final.T


def body(volume, tf_table, view_code):
    depth_size, band_size = lax.axis_size("depth"), lax.axis_size("band")
    slabs, rows, extent = volume.shape
    wide = rows + 2 * MARGIN
    stations = depth_size // 4
    chunk = extent // stations
    strip = chunk // 4
    reach = chunk + 2 * MARGIN
    piece = strip + 2 * MARGIN
    slots = 1 if band_size == 2 else 2
    bf16, f32 = jnp.bfloat16, jnp.float32
    vmem = pl.BlockSpec(memory_space=pltpu.VMEM)
    dma = pltpu.SemaphoreType.DMA
    out = pl.pallas_call(
        functools.partial(kernel, (depth_size, band_size)),
        out_shape=jax.ShapeDtypeStruct((VIEWS, LANES, strip), f32),
        in_specs=[pl.BlockSpec(memory_space=pltpu.SMEM), vmem, vmem],
        out_specs=vmem,
        scratch_shapes=[
            pltpu.VMEM((2, slabs, MARGIN, extent), bf16),
            pltpu.VMEM((slots, slabs, MARGIN, extent), bf16),
            pltpu.VMEM((slabs, 4 * wide, extent + 2 * PAD), bf16),
            pltpu.VMEM((slabs, VIEWS * reach, chunk + 2 * PAD), bf16),
            pltpu.VMEM((VIEWS * slabs, 4 * wide, 2 * LANES), bf16),
            pltpu.VMEM((VIEWS, slabs, reach, 2 * LANES), f32),
            pltpu.VMEM((stations, VIEWS, reach, LANES), f32),
            pltpu.VMEM((stations, VIEWS, 2, piece, LANES), bf16),
            pltpu.VMEM((stations, VIEWS, 2, piece, LANES), bf16),
            pltpu.VMEM((stations, VIEWS, piece, LANES), bf16),
            pltpu.VMEM((stations, VIEWS, piece, LANES), bf16),
            pltpu.VMEM((stations, VIEWS, piece, LANES), f32),
            pltpu.VMEM((stations, VIEWS, piece, LANES), bf16),
            pltpu.VMEM((stations, VIEWS, piece, LANES), bf16),
            pltpu.VMEM((VIEWS, piece, LANES), f32),
            dma((2, 3)), dma((slots, 3)),
            dma((stations,)), dma((stations,)),
            dma((stations,)), dma((stations,)),
            dma((stations,)), dma((stations,)),
        ],
        compiler_params=pltpu.CompilerParams(collective_id=0, has_side_effects=True),
    )(view_code, volume, tf_table)
    return out.reshape(VIEWS, 4, rows, strip).transpose(0, 3, 1, 2)


def solution(mesh):
    P = jax.sharding.PartitionSpec
    placed = (P("depth", "band", None), P(), P())
    return jax.shard_map(
        body, mesh=mesh, in_specs=placed, out_specs=P(None, "depth", None, "band"), check_vma=False
    )
```
